32 devices in a mesh: groups: 2 (over x), track: 8 (over z, y), sub: 2 (over core).
Axes of the slice: x: 2, y: 2, z: 4, core: 2. Of those that a mesh axis runs over, the one named last changes fastest.
Arguments:
- tokens: bfloat16 [512, 128, 384], P(('groups', 'track', 'sub')), parts along dimension 0, may hold values from -6 to 6
- visible: int32 [512, 2], P(('groups', 'track', 'sub')), parts along dimension 0, may hold values from 0 to 128, as said below
- time_attn: bfloat16 [4, 384, 384], replicated, may hold values from -0.3125 to 0.3125
- mlp_in: bfloat16 [384, 1536], replicated, may hold values from -0.3125 to 0.3125
- mlp_out: bfloat16 [1536, 384], replicated, may hold values from -0.15625 to 0.15625
- virt_attn: bfloat16 [3, 4, 384, 384], replicated, may hold values from -0.3125 to 0.3125
- virtual: bfloat16 [64, 384], replicated, may hold values from -6 to 6
Outputs:
- updated: bfloat16 [512, 128, 384], P(('groups', 'track', 'sub')), parts along dimension 0
The draws below stay inside these ranges and needn't reach their ends.
There are 2 independent parts, one for each index of `groups`. The reference program is written for one: setup_inputs(seed, part) draws one part's arguments, and reference() takes and returns one part's arrays. A program takes and returns all parts, laid end to end along the dimension named above; an argument that names none is the same for every part. Nothing has to cross between parts.
Inputs may be any that keep to these rules, and one draw needn't show every extreme that they name: visible[n, 0] < visible[n, 1]; the first track of every block of 16 tracks is visible in all 128 frames.
All inputs are finite; a program needn't handle non-finite values.
Results may differ from the reference program's by a relative error of at most 0.0095.
Values may be sent and summed in bfloat16 or wider, within the bound.
A program may use at most 128 MiB of HBM per device.

```python
import math
import jax
import jax.numpy as jnp
from jax import lax

D = 384
FF = 1536
HEADS = 8
VIRT = 64
TRK_DEV = 16
TRACKS = 256
FRAMES = 128


def draw_visible(key, part):
    key_limit, key_length, key_offset = jax.random.split(key, 3)
    blocks = TRACKS // TRK_DEV
    limits = jax.random.randint(key_limit, (blocks, 1), max(FRAMES // 4, 1), FRAMES + 1)
    lengths = jax.random.randint(key_length, (blocks, TRK_DEV), 0, 1048576) % limits + 1
    column = jnp.arange(TRK_DEV, dtype=jnp.int32)[None, :]
    lengths = jnp.where(column == 0, FRAMES, lengths).reshape(TRACKS)
    offsets = jax.random.randint(key_offset, (TRACKS,), 0, 1048576) % (FRAMES - lengths + 1)
    return jnp.stack([offsets, offsets + lengths], axis=1).astype(jnp.int32)


def shard_levels(key, dims, shards, smallest, top_value):
    gain, own = 1.0, jax.random.fold_in(key, 6)
    for axis_at, shards_of in shards:
        heights = jnp.exp(jax.random.uniform(jax.random.fold_in(own, axis_at), (shards_of,), jnp.float32, smallest / len(shards), top_value / len(shards)))
        gain = gain * jnp.repeat(heights, dims[axis_at] // shards_of).reshape([-1 if axis == axis_at else 1 for axis in range(len(dims))])
    return gain


def gaussian(stream_key, dims, deviation, limit, cuts=(), kind=jnp.bfloat16):
    values = deviation * jax.random.normal(stream_key, dims, jnp.float32)
    if cuts:
        values = values * shard_levels(stream_key, dims, cuts, -0.22, 0.18)
    return jnp.clip(values, -limit, limit).astype(kind)


def setup_inputs(seed: int = 0, part: int = 0) -> dict:
    splits = jax.random.split(jax.random.key(seed), 8)
    part_keys = jax.random.split(jax.random.fold_in(splits[7], part), 8)
    tokens = gaussian(part_keys[0], (TRACKS, FRAMES, D), 1.0, 6.0, ((0, 16),))
    visible = draw_visible(jax.random.fold_in(jax.random.fold_in(splits[7], part), 71), part)
    time_attn = gaussian(splits[2], (4, D, D), D ** -0.5, 0.3125)
    mlp_in = gaussian(splits[3], (D, FF), D ** -0.5, 0.3125)
    mlp_out = gaussian(splits[4], (FF, D), FF ** -0.5, 0.15625)
    virt_attn = gaussian(splits[5], (3, 4, D, D), D ** -0.5, 0.3125)
    virtual = gaussian(splits[6], (VIRT, D), 1.0, 6.0)
    return dict(tokens=tokens, visible=visible, time_attn=time_attn, mlp_in=mlp_in, mlp_out=mlp_out, virt_attn=virt_attn, virtual=virtual)


def layer_norm(values):
    wide = values.astype(jnp.float32)
    center = wide - lax.optimization_barrier(jnp.mean(wide, axis=-1, keepdims=True))
    spread = lax.optimization_barrier(jnp.mean(center * center, axis=-1, keepdims=True))
    return (center * lax.rsqrt(spread + 1e-05)).astype(jnp.bfloat16)

def project(values, matrix):
    return jnp.dot(values, matrix, preferred_element_type=jnp.float32)

def attend(queries, key_rows, value_rows, mask):
    n_batch, n_query, feature = queries.shape
    n_keys = key_rows.shape[1]
    head_size = feature // HEADS
    query_h = queries.reshape(n_batch, n_query, HEADS, head_size).astype(jnp.float32)
    key_h = key_rows.reshape(n_batch, n_keys, HEADS, head_size).astype(jnp.float32)
    value_h = value_rows.reshape(n_batch, n_keys, HEADS, head_size).astype(jnp.float32)
    scores = jnp.einsum('bqhe,bkhe->bhqk', query_h, key_h) * (1.0 / math.sqrt(head_size))
    if mask is not None:
        scores = jnp.where(mask, scores, -1e+30)
    weights = jax.nn.softmax(scores, axis=-1).astype(jnp.bfloat16)
    mixed = jnp.einsum('bhqk,bkhe->bqhe', weights.astype(jnp.float32), value_h).astype(jnp.bfloat16)
    return mixed.reshape(n_batch, n_query, feature)

def time_block(tokens, visible, time_attn, mlp_in, mlp_out):
    frame_ids = jnp.arange(tokens.shape[1], dtype=jnp.int32)
    seen = (frame_ids[None, :] >= visible[:, 0:1]) & (frame_ids[None, :] < visible[:, 1:2])
    vis = seen.astype(jnp.float32)[:, :, None]
    normed = layer_norm(tokens)
    queries = project(normed, time_attn[0]).astype(jnp.bfloat16)
    key_rows = project(normed, time_attn[1]).astype(jnp.bfloat16)
    value_rows = project(normed, time_attn[2]).astype(jnp.bfloat16)
    mixed = attend(queries, key_rows, value_rows, seen[:, None, None, :])
    first = tokens.astype(jnp.float32) + vis * project(mixed, time_attn[3])
    hidden = jax.nn.gelu(project(layer_norm(first), mlp_in), approximate=True).astype(jnp.bfloat16)
    return (first + vis * project(hidden, mlp_out)).astype(jnp.bfloat16)

def frame_block(framed, virt_attn, virtual):
    n_frames = framed.shape[0]
    normed = layer_norm(framed)
    key_c = project(normed, virt_attn[0, 1]).astype(jnp.bfloat16)
    value_c = project(normed, virt_attn[0, 2]).astype(jnp.bfloat16)
    query_c = project(layer_norm(virtual), virt_attn[0, 0]).astype(jnp.bfloat16)
    query_c = jnp.broadcast_to(query_c[None], (n_frames,) + query_c.shape)
    cross = attend(query_c, key_c, value_c, None)
    first = virtual.astype(jnp.float32)[None] + project(cross, virt_attn[0, 3])
    normed_w = layer_norm(first)
    query_s = project(normed_w, virt_attn[1, 0]).astype(jnp.bfloat16)
    key_s = project(normed_w, virt_attn[1, 1]).astype(jnp.bfloat16)
    value_s = project(normed_w, virt_attn[1, 2]).astype(jnp.bfloat16)
    second = first + project(attend(query_s, key_s, value_s, None), virt_attn[1, 3])
    normed_b = layer_norm(second)
    key_b = project(normed_b, virt_attn[2, 1]).astype(jnp.bfloat16)
    value_b = project(normed_b, virt_attn[2, 2]).astype(jnp.bfloat16)
    query_b = project(normed, virt_attn[2, 0]).astype(jnp.bfloat16)
    back = attend(query_b, key_b, value_b, None)
    return (framed.astype(jnp.float32) + project(back, virt_attn[2, 3])).astype(jnp.bfloat16)

def reference(tokens, visible, time_attn, mlp_in, mlp_out, virt_attn, virtual):
    block = 16
    grouped = tokens.reshape(TRACKS // block, block, FRAMES, D)
    grouped_vis = visible.reshape(TRACKS // block, block, 2)
    after = lax.map(lambda pair: time_block(pair[0], pair[1], time_attn, mlp_in, mlp_out), (grouped, grouped_vis))
    after = after.reshape(TRACKS, FRAMES, D)
    framed = jnp.swapaxes(after, 0, 1).reshape(FRAMES, 1, TRACKS, D)
    result = lax.map(lambda single: frame_block(single, virt_attn, virtual), framed)
    return jnp.swapaxes(result.reshape(FRAMES, TRACKS, D), 0, 1)
```

```python
import functools
import math

import jax
import jax.numpy as jnp
from jax import lax
from jax.experimental import pallas as pl
from jax.experimental.pallas import tpu as pltpu
from jax.sharding import PartitionSpec as P

HEADS = 8
F32 = jnp.float32
BF16 = jnp.bfloat16


def layer_norm(values):
    wide = values.astype(F32)
    center = wide - jnp.mean(wide, axis=-1, keepdims=True)
    spread = jnp.mean(center * center, axis=-1, keepdims=True)
    return (center * lax.rsqrt(spread + 1e-05)).astype(BF16)


def project(values, matrix):
    return jnp.dot(values, matrix, preferred_element_type=F32)


def product(left, right, left_dim, right_dim):
    dims = (((left_dim,), (right_dim,)), ((), ()))
    return lax.dot_general(left, right, dims, preferred_element_type=F32)


def head_masks(feature, kind):
    size = feature // HEADS
    lanes = lax.broadcasted_iota(jnp.int32, (1, feature), 1)
    return [
        jnp.where((lanes >= head * size) & (lanes < (head + 1) * size), 1.0, 0.0).astype(kind)
        for head in range(HEADS)
    ]


def spread_heads(rows, masks):
    return jnp.concatenate([rows * mask for mask in masks], axis=0)


def time_step(tokens, first_frame, end_frame, attn_ref, in_ref, out_ref, ones_ref, ready):
    tracks, frames, feature = tokens.shape
    scale = 1.0 / math.sqrt(feature // HEADS)
    masks = head_masks(feature, BF16)
    wide = tokens.reshape(tracks * frames, feature).astype(F32)
    normed = layer_norm(wide)
    queries = project(normed, attn_ref[0]).astype(BF16)
    keys = project(normed, attn_ref[1]).astype(BF16)
    values = project(normed, attn_ref[2]).astype(BF16)
    lane = lax.broadcasted_iota(jnp.int32, (1, frames), 1)
    row = lax.broadcasted_iota(jnp.int32, (frames, feature), 0)
    mixed, vis = [], []
    for track in range(tracks):
        part = slice(track * frames, (track + 1) * frames)
        seen = (lane >= first_frame[track]) & (lane < end_frame[track])
        scores = product(queries[part], spread_heads(keys[part], masks), 1, 1)
        weights = []
        for head in range(HEADS):
            own = scores[:, head * frames : (head + 1) * frames] * scale
            own = jnp.where(seen, own, -1e30)
            top = jnp.max(own, axis=-1, keepdims=True)
            weights.append(jnp.exp(own - top).astype(BF16))
        weights = jnp.concatenate(weights, axis=1)
        summed = project(weights, spread_heads(values[part], masks))
        total = project(weights, ones_ref[...])
        mixed.append((summed / total).astype(BF16))
        shown = (row >= first_frame[track]) & (row < end_frame[track])
        vis.append(jnp.where(shown, 1.0, 0.0).astype(F32))
    mixed = jnp.concatenate(mixed, axis=0)
    vis = jnp.concatenate(vis, axis=0)
    first = wide + vis * project(mixed, attn_ref[3])
    ready()
    hidden = jax.nn.gelu(project(layer_norm(first), in_ref[...]), approximate=True).astype(BF16)
    return first + vis * project(hidden, out_ref[...])


def fill_ones(ones_ref, feature):
    rows = ones_ref.shape[0] // HEADS
    for head, mask in enumerate(head_masks(feature, F32)):
        ones_ref[head * rows : (head + 1) * rows, :] = jnp.broadcast_to(mask, (rows, feature)).astype(BF16)


def few_queries(spread_queries, keys, values, masks):
    feature = keys.shape[1]
    scores = product(spread_queries, keys, 1, 1) * (1.0 / math.sqrt(feature // HEADS))
    top = jnp.max(scores, axis=-1, keepdims=True)
    weights = jnp.exp(scores - top)
    total = jnp.sum(weights, axis=-1, keepdims=True)
    summed = project(weights.astype(BF16), values) / total
    count = spread_queries.shape[0] // HEADS
    mixed = summed[:count] * masks[0]
    for head in range(1, HEADS):
        mixed = mixed + summed[head * count : (head + 1) * count] * masks[head]
    return mixed.astype(BF16)


def frame_step(wide, key_c, value_c, query_b, attn_ref, virtual_ref, query_ref, ones_ref):
    frames, tracks, feature = wide.shape
    n_virtual = virtual_ref.shape[0]
    scale = 1.0 / math.sqrt(feature // HEADS)
    masks = head_masks(feature, BF16)
    wide_masks = head_masks(feature, F32)
    wide = wide.reshape(frames * tracks, feature).astype(F32)
    virtual_part = [slice(f * n_virtual, (f + 1) * n_virtual) for f in range(frames)]
    cross = [few_queries(query_ref[...], key_c[f], value_c[f], wide_masks) for f in range(frames)]
    base = jnp.concatenate([virtual_ref[...].astype(F32)] * frames, axis=0)
    first = base + project(jnp.concatenate(cross, axis=0), attn_ref[0, 3])
    normed_w = layer_norm(first)
    query_s = project(normed_w, attn_ref[1, 0]).astype(BF16)
    key_s = project(normed_w, attn_ref[1, 1]).astype(BF16)
    value_s = project(normed_w, attn_ref[1, 2]).astype(BF16)
    among = [
        few_queries(spread_heads(query_s[part], masks), key_s[part], value_s[part], wide_masks)
        for part in virtual_part
    ]
    second = first + project(jnp.concatenate(among, axis=0), attn_ref[1, 3])
    normed_b = layer_norm(second)
    key_b = project(normed_b, attn_ref[2, 1]).astype(BF16)
    value_b = project(normed_b, attn_ref[2, 2]).astype(BF16)
    back = []
    for frame in range(frames):
        part = virtual_part[frame]
        scores = product(spread_heads(key_b[part], masks), query_b[frame], 1, 1) * scale
        scores = scores.reshape(HEADS, n_virtual, tracks)
        top = jnp.max(scores, axis=1, keepdims=True)
        weights = jnp.exp(scores - top).astype(BF16).reshape(HEADS * n_virtual, tracks)
        summed = product(weights, spread_heads(value_b[part], masks), 0, 0)
        total = product(weights, ones_ref[...], 0, 0)
        back.append((summed / total).astype(BF16))
    return wide + project(jnp.concatenate(back, axis=0), attn_ref[2, 3])


def interleave(first, second, count):
    frames, feature = first.shape
    each = frames // count
    first = first.reshape(count, each, feature)
    second = second.reshape(count, each, feature)
    row = lax.broadcasted_iota(jnp.int32, first.shape, 1)
    short = each // 2
    early = jnp.where(row < short, first, pltpu.roll(second, short, 1))
    late = jnp.where(row < short, pltpu.roll(first, short, 1), second)
    return early, late


class Exchange:
    def __init__(self, shape):
        self.n_sub = shape["sub"]
        self.count = shape["track"] * shape["sub"]
        self.me = lax.axis_index("track") * self.n_sub + lax.axis_index("sub")
        self.offsets = sorted(range(1, self.count), key=lambda j: abs(2 * j - self.count))

    def device(self, peer):
        return {"track": peer // self.n_sub, "sub": peer % self.n_sub}

    def greet(self):
        barrier = pltpu.get_barrier_semaphore()
        for offset in self.offsets:
            pl.semaphore_signal(
                barrier,
                inc=1,
                device_id=self.device(lax.rem(self.me + offset, self.count)),
                device_id_type=pl.DeviceIdType.MESH,
            )

    def admit(self):
        pl.semaphore_wait(pltpu.get_barrier_semaphore(), self.count - 1)

    def send(self, source_of, target, send_sem, recv_sem, local_sem):
        for offset in self.offsets:
            peer = lax.rem(self.me + offset, self.count)
            pltpu.make_async_remote_copy(
                src_ref=source_of(peer),
                dst_ref=target,
                send_sem=send_sem,
                recv_sem=recv_sem,
                device_id=self.device(peer),
                device_id_type=pl.DeviceIdType.MESH,
            ).start()
        pltpu.make_async_copy(source_of(self.me), target, local_sem).start()


def await_bytes(ref, sem):
    pltpu.make_async_copy(ref, ref, sem).wait()


def layer_kernel(
    shape, n_time, frame_group,
    vis_ref, tok_ref, attn_ref, in_hbm, out_hbm, virt_hbm, virtual_ref, dest_ref,
    time_ones, frame_ones, sort_ref, pair_ref, home_ref, query_ref, in_ref, out_ref, virt_ref,
    slab, inbox, x_ref, key_ref, value_ref, qb_ref, outbox,
    in_sem, out_sem, weight_sem, send1, recv1, local1, send2, recv2, local2,
):
    step = pl.program_id(0)
    group, frames, feature = tok_ref.shape
    exchange = Exchange(shape)
    count = exchange.count
    each = frames // count
    chunk = count * group
    tracks = chunk * n_time
    own_tracks = n_time * group
    lag = n_time - 2
    n_whole = n_time // 2
    early_at = lag + n_whole
    frame_at = early_at + (n_time - n_whole) // 2
    late_at = frame_at + each // 2 // frame_group
    late_frame_at = late_at + (n_time - n_whole) // 2

    @pl.when(step == 0)
    def _():
        pltpu.make_async_copy(in_hbm, in_ref, in_sem).start()
        pltpu.make_async_copy(out_hbm, out_ref, out_sem).start()
        exchange.greet()
        pltpu.make_async_copy(virt_hbm, virt_ref, weight_sem).start()
        fill_ones(time_ones, feature)

    def send_half(index, half):
        slot = index if half == 0 else index - n_whole + n_time
        exchange.send(
            lambda peer: slab.at[index, peer, half],
            inbox.at[index, exchange.me, half],
            send1, recv1.at[slot], local1.at[slot],
        )

    def ready():
        @pl.when(step == 0)
        def _():
            pltpu.make_async_copy(in_hbm, in_ref, in_sem).wait()
            pltpu.make_async_copy(out_hbm, out_ref, out_sem).wait()

    @pl.when(step < n_time)
    def _():
        begin = [vis_ref[0, step * group + i] for i in range(group)]
        end = [vis_ref[1, step * group + i] for i in range(group)]
        after = time_step(tok_ref[...], begin, end, attn_ref, in_ref, out_ref, time_ones, ready)
        early, late = interleave(after[:frames], after[frames:], count)
        slab[step, :, 0] = early.astype(BF16)
        slab[step, :, 1] = late.astype(BF16)

        @pl.when(step == 0)
        def _():
            exchange.admit()

        @pl.when(step < n_whole)
        def _():
            exchange.send(
                lambda peer: slab.at[step, peer], inbox.at[step, exchange.me], send1, recv1.at[step], local1.at[step]
            )

        @pl.when(step >= n_whole)
        def _():
            send_half(step, 0)

        @pl.when(step == n_time - 1)
        def _():
            for index in range(n_whole, n_time):
                send_half(index, 1)

    @pl.when(step == lag)
    def _():
        pltpu.make_async_copy(virt_hbm, virt_ref, weight_sem).wait()
        fill_ones(frame_ones, feature)
        query = project(layer_norm(virtual_ref[...]), virt_ref[0, 0]).astype(BF16)
        query_ref[...] = spread_heads(query, head_masks(feature, BF16))
        row = lax.broadcasted_iota(jnp.int32, (chunk * each, chunk * each), 0)
        col = lax.broadcasted_iota(jnp.int32, (chunk * each, chunk * each), 1)
        frame, track, short = row // chunk, row % chunk, each // 2
        place = track // group * each * group + frame // short * short * group + track % group * short + frame % short
        sort_ref[...] = jnp.where(col == place, 1.0, 0.0).astype(BF16)
        track = row % (2 * chunk)
        frame = row // (2 * chunk)
        place = track // group * short * group + track % group * short + frame
        pair_ref[...] = jnp.where(col == place, 1.0, 0.0).astype(BF16)
        row = lax.broadcasted_iota(jnp.int32, (tracks, tracks), 0)
        col = lax.broadcasted_iota(jnp.int32, (tracks, tracks), 1)
        track = row % own_tracks
        place = track // group * chunk + row // own_tracks * group + track % group
        home_ref[...] = jnp.where(col == place, 1.0, 0.0).astype(BF16)

    def keep(rows, place, part):
        normed = layer_norm(rows)
        shape_kept = (part.size, rows.shape[0] // part.size, feature)
        for ref, values in (
            (x_ref, rows),
            (key_ref, project(normed, virt_ref[0, 1]).astype(BF16)),
            (value_ref, project(normed, virt_ref[0, 2]).astype(BF16)),
            (qb_ref, project(normed, virt_ref[2, 0]).astype(BF16)),
        ):
            ref[part, place] = values.reshape(shape_kept)

    @pl.when((step >= lag) & (step < early_at))
    def _():
        index = step - lag
        await_bytes(inbox.at[index, pl.ds(0, count - 1)], recv1.at[index])
        await_bytes(inbox.at[index, 0], local1.at[index])
        rows = inbox[index].reshape(chunk * each, feature)
        rows = project(sort_ref[...], rows).astype(BF16)
        keep(rows, pl.ds(pl.multiple_of(index * chunk, chunk), chunk), pl.ds(0, each))

    def arrive_half(pair, half):
        index = n_whole + 2 * pair
        blocks = []
        for i in range(2):
            slot = index + i if half == 0 else index + i - n_whole + n_time
            await_bytes(inbox.at[index + i, pl.ds(0, count - 1), half], recv1.at[slot])
            await_bytes(inbox.at[index + i, 0, half], local1.at[slot])
            blocks.append(inbox[index + i, :, half].reshape(chunk * each // 2, feature))
        rows = project(pair_ref[...], jnp.concatenate(blocks, axis=0)).astype(BF16)
        place = pl.ds(pl.multiple_of(index * chunk, 2 * chunk), 2 * chunk)
        keep(rows, place, pl.ds(half * (each // 2), each // 2))

    @pl.when((step >= early_at) & (step < frame_at))
    def _():
        arrive_half(step - early_at, 0)

    @pl.when((step >= late_at) & (step < late_frame_at))
    def _():
        arrive_half(step - late_at, 1)

    @pl.when(((step >= frame_at) & (step < late_at)) | (step >= late_frame_at))
    def _():
        first = jnp.where(step < late_at, step - frame_at, step - late_frame_at + late_at - frame_at) * frame_group
        part = pl.ds(first, frame_group)
        after = frame_step(
            x_ref[part], key_ref[part], value_ref[part], qb_ref[part], virt_ref, virtual_ref, query_ref, frame_ones
        ).astype(BF16)
        for f in range(frame_group):
            block = project(home_ref[...], after[f * tracks : (f + 1) * tracks]).astype(BF16)
            outbox[:, first + f] = block.reshape(count, own_tracks, feature)
        exchange.send(
            lambda peer: outbox.at[peer, part],
            dest_ref.at[pl.ds(exchange.me * each + first, frame_group)],
            send2,
            recv2,
            local2,
        )

    @pl.when(step == pl.num_programs(0) - 1)
    def _():
        await_bytes(slab.at[:, pl.ds(0, count - 1)], send1)
        others = dest_ref.at[pl.ds(0, (count - 1) * each)]
        await_bytes(dest_ref.at[pl.ds(0, each)], local2)
        await_bytes(others, send2)
        await_bytes(others, recv2)


WHOLE = pl.BlockSpec(memory_space=pltpu.VMEM)
ANY = pl.BlockSpec(memory_space=pl.ANY)
LIMIT = 60 * 1024 * 1024


def shards(shape, tokens, visible, time_attn, mlp_in, mlp_out, virt_attn, virtual):
    own_tracks, frames, feature = tokens.shape
    n_virtual = virtual.shape[0]
    count = shape["track"] * shape["sub"]
    group, frame_group = 2, 1
    each = frames // count
    n_time = own_tracks // group
    tracks = count * own_tracks
    chunk = count * group
    by_frame = pltpu.VMEM((each, tracks, feature), BF16)
    dma = pltpu.SemaphoreType.DMA
    result = pl.pallas_call(
        functools.partial(layer_kernel, shape, n_time, frame_group),
        grid=(n_time + n_time - 2 + each // frame_group,),
        in_specs=[
            pl.BlockSpec(memory_space=pltpu.SMEM),
            pl.BlockSpec((group, frames, feature), lambda i: (jnp.minimum(i, n_time - 1), 0, 0)),
            WHOLE, ANY, ANY, ANY, WHOLE,
        ],
        out_specs=ANY,
        out_shape=jax.ShapeDtypeStruct((frames, own_tracks, feature), BF16),
        scratch_shapes=[
            pltpu.VMEM((HEADS * frames, feature), BF16),
            pltpu.VMEM((HEADS * n_virtual, feature), BF16),
            pltpu.VMEM((chunk * each, chunk * each), BF16),
            pltpu.VMEM((chunk * each, chunk * each), BF16),
            pltpu.VMEM((tracks, tracks), BF16),
            pltpu.VMEM((HEADS * n_virtual, feature), BF16),
            pltpu.VMEM(mlp_in.shape, BF16),
            pltpu.VMEM(mlp_out.shape, BF16),
            pltpu.VMEM(virt_attn.shape, BF16),
            pltpu.VMEM((n_time, count, 2, each, feature), BF16),
            pltpu.VMEM((n_time, count, 2, each, feature), BF16),
            by_frame, by_frame, by_frame, by_frame,
            pltpu.VMEM((count, each, own_tracks, feature), BF16),
            dma, dma, dma, dma, dma((2 * n_time,)), dma((2 * n_time,)), dma, dma, dma,
        ],
        compiler_params=pltpu.CompilerParams(vmem_limit_bytes=LIMIT, collective_id=0, has_side_effects=True),
    )(visible.T, tokens, time_attn, mlp_in, mlp_out, virt_attn, virtual)
    return jnp.swapaxes(result, 0, 1)


def solution(mesh):
    placed = (
        P(("groups", "track", "sub"), None, None),
        P(("groups", "track", "sub"), None),
        P(),
        P(),
        P(),
        P(),
        P(),
    )
    return jax.shard_map(
        functools.partial(shards, dict(mesh.shape)),
        mesh=mesh,
        in_specs=placed,
        out_specs=P(("groups", "track", "sub"), None, None),
        check_vma=False,
    )
```

```python
import functools
import math

import jax
import jax.numpy as jnp
from jax import lax
from jax.experimental import pallas as pl
from jax.experimental.pallas import tpu as pltpu
from jax.sharding import PartitionSpec as P

HEADS = 8
LANES = 128
LOG2E = math.log2(math.e)
F32 = jnp.float32
BF16 = jnp.bfloat16


def layer_norm(values):
    wide = values.astype(F32)
    center = wide - jnp.mean(wide, axis=-1, keepdims=True)
    spread = jnp.mean(center * center, axis=-1, keepdims=True)
    return (center * lax.rsqrt(spread + 1e-05)).astype(BF16)


def project(values, matrix):
    return jnp.dot(values, matrix, preferred_element_type=F32)


def product(left, right, left_dim, right_dim):
    dims = (((left_dim,), (right_dim,)), ((), ()))
    return lax.dot_general(left, right, dims, preferred_element_type=F32)


def head_masks(feature, kind):
    size = feature // HEADS
    lanes = lax.broadcasted_iota(jnp.int32, (1, feature), 1)
    return [
        jnp.where((lanes >= head * size) & (lanes < (head + 1) * size), 1.0, 0.0).astype(kind)
        for head in range(HEADS)
    ]


def head_groups(feature):
    middle = feature // 2
    heads = HEADS // 2
    return (
        (range(heads), slice(0, -(-middle // LANES) * LANES)),
        (range(heads, HEADS), slice(middle // LANES * LANES, feature)),
    )


def spread_heads(rows, masks, group):
    heads, lanes = group
    return jnp.concatenate([rows[:, lanes] * masks[head][:, lanes] for head in heads], axis=0)


def join_groups(low, high, feature):
    (_, first), (_, second) = head_groups(feature)
    shared = first.stop - second.start
    if not shared:
        return jnp.concatenate([low, high], axis=1)
    middle = low[:, second.start :] + high[:, :shared]
    return jnp.concatenate([low[:, : second.start], middle, high[:, shared:]], axis=1)


def time_step(tokens, first_frame, end_frame, attn_ref, in_ref, out_ref, ones_ref, ready):
    tracks, frames, feature = tokens.shape
    scale = LOG2E / math.sqrt(feature // HEADS)
    groups = head_groups(feature)
    masks = head_masks(feature, BF16)
    wide = tokens.reshape(tracks * frames, feature).astype(F32)
    normed = layer_norm(wide)
    queries = project(normed, attn_ref[0]).astype(BF16)
    keys = project(normed, attn_ref[1]).astype(BF16)
    values = project(normed, attn_ref[2]).astype(BF16)
    lane = lax.broadcasted_iota(jnp.int32, (1, frames), 1)
    row = lax.broadcasted_iota(jnp.int32, (frames, feature), 0)
    mixed, vis = [], []
    for track in range(tracks):
        part = slice(track * frames, (track + 1) * frames)
        seen = (lane >= first_frame[track]) & (lane < end_frame[track])
        outs = []
        for at, group in enumerate(groups):
            heads, lanes = group
            scores = product(queries[part, lanes], spread_heads(keys[part], masks, group), 1, 1)
            weights = []
            for head in range(len(heads)):
                own = scores[:, head * frames : (head + 1) * frames]
                own = jnp.where(seen, own, -1e30)
                top = jnp.max(own, axis=-1, keepdims=True)
                weights.append(jnp.exp2((own - top) * scale).astype(BF16))
            weights = jnp.concatenate(weights, axis=1)
            outs.append(project(weights, spread_heads(values[part], masks, group)))
            outs.append(project(weights, ones_ref[at]))
        summed = join_groups(outs[0], outs[2], feature)
        total = join_groups(outs[1], outs[3], feature)
        mixed.append((summed / total).astype(BF16))
        shown = (row >= first_frame[track]) & (row < end_frame[track])
        vis.append(jnp.where(shown, 1.0, 0.0).astype(F32))
    mixed = jnp.concatenate(mixed, axis=0)
    vis = jnp.concatenate(vis, axis=0)
    first = wide + vis * project(mixed, attn_ref[3])
    ready()
    hidden = jax.nn.gelu(project(layer_norm(first), in_ref[...]), approximate=True).astype(BF16)
    return first + vis * project(hidden, out_ref[...])


def fill_ones(ones_ref, feature):
    rows = ones_ref.shape[1] // (HEADS // 2)
    masks = head_masks(feature, F32)
    for at, (heads, lanes) in enumerate(head_groups(feature)):
        for place, head in enumerate(heads):
            mask = masks[head][:, lanes]
            ones_ref[at, place * rows : (place + 1) * rows, :] = jnp.broadcast_to(
                mask, (rows, mask.shape[1])
            ).astype(BF16)


def few_queries(spread_queries, keys, values, wide_masks):
    feature = keys.shape[1]
    scale = LOG2E / math.sqrt(feature // HEADS)
    outs = []
    for queries, (heads, lanes) in zip(spread_queries, head_groups(feature)):
        scores = product(queries, keys[:, lanes], 1, 1)
        top = jnp.max(scores, axis=-1, keepdims=True)
        weights = jnp.exp2((scores - top) * scale)
        total = jnp.sum(weights, axis=-1, keepdims=True)
        summed = project(weights.astype(BF16), values[:, lanes]) * (1.0 / total)
        count = queries.shape[0] // len(heads)
        mixed = 0.0
        for place, head in enumerate(heads):
            mixed = mixed + summed[place * count : (place + 1) * count] * wide_masks[head][:, lanes]
        outs.append(mixed)
    return join_groups(outs[0], outs[1], feature).astype(BF16)


def virtual_step(key_c, value_c, attn_ref, virtual_ref, query_ref):
    frames, tracks, feature = key_c.shape
    n_virtual = virtual_ref.shape[0]
    masks = head_masks(feature, BF16)
    wide_masks = head_masks(feature, F32)
    groups = head_groups(feature)
    virtual_part = [slice(f * n_virtual, (f + 1) * n_virtual) for f in range(frames)]
    cross = [few_queries((query_ref[0], query_ref[1]), key_c[f], value_c[f], wide_masks) for f in range(frames)]
    base = jnp.concatenate([virtual_ref[...].astype(F32)] * frames, axis=0)
    first = base + project(jnp.concatenate(cross, axis=0), attn_ref[0, 3])
    normed_w = layer_norm(first)
    query_s = project(normed_w, attn_ref[1, 0]).astype(BF16)
    key_s = project(normed_w, attn_ref[1, 1]).astype(BF16)
    value_s = project(normed_w, attn_ref[1, 2]).astype(BF16)
    among = [
        few_queries([spread_heads(query_s[part], masks, group) for group in groups], key_s[part], value_s[part], wide_masks)
        for part in virtual_part
    ]
    second = first + project(jnp.concatenate(among, axis=0), attn_ref[1, 3])
    return layer_norm(second)


def back_step(wide, query_b, normed_b, attn_ref):
    frames, tracks, feature = wide.shape
    n_virtual = normed_b.shape[0] // frames
    scale = LOG2E / math.sqrt(feature // HEADS)
    masks = head_masks(feature, BF16)
    wide = wide.reshape(frames * tracks, feature).astype(F32)
    key_b = project(normed_b, attn_ref[2, 1]).astype(BF16)
    value_b = project(normed_b, attn_ref[2, 2]).astype(BF16)
    back = []
    for frame in range(frames):
        part = slice(frame * n_virtual, (frame + 1) * n_virtual)
        outs = []
        for group in head_groups(feature):
            heads, lanes = group
            scores = product(spread_heads(key_b[part], masks, group), query_b[frame][:, lanes], 1, 1)
            scores = scores.reshape(len(heads), n_virtual, tracks)
            top = jnp.max(scores, axis=1, keepdims=True)
            weights = jnp.exp2((scores - top) * scale)
            weights = weights * (1.0 / jnp.sum(weights, axis=1, keepdims=True))
            weights = weights.astype(BF16).reshape(len(heads) * n_virtual, tracks)
            outs.append(product(weights, spread_heads(value_b[part], masks, group), 0, 0))
        back.append(join_groups(outs[0], outs[1], feature).astype(BF16))
    return wide + project(jnp.concatenate(back, axis=0), attn_ref[2, 3])


def interleave(first, second, count):
    frames, feature = first.shape
    each = frames // count
    first = first.reshape(count, each, feature)
    second = second.reshape(count, each, feature)
    row = lax.broadcasted_iota(jnp.int32, first.shape, 1)
    short = each // 2
    early = jnp.where(row < short, first, pltpu.roll(second, short, 1))
    late = jnp.where(row < short, pltpu.roll(first, short, 1), second)
    return early, late


class Exchange:
    def __init__(self, shape):
        self.n_sub = shape["sub"]
        self.count = shape["track"] * shape["sub"]
        self.side = self.count // 2
        me = lax.axis_index("track") * self.n_sub + lax.axis_index("sub")
        self.local = lax.rem(me, self.side)
        self.here = me - self.local
        self.there = self.side - self.here
        self.offsets = sorted(range(1, self.side), key=lambda j: abs(2 * j - self.side))

    def near(self, offset):
        return lax.rem(self.local + offset, self.side)

    def device(self, peer):
        return {"track": peer // self.n_sub, "sub": peer % self.n_sub}

    def greet(self):
        barrier = pltpu.get_barrier_semaphore()
        peers = [self.there + self.near(j) for j in range(self.side)]
        peers += [self.here + self.near(j) for j in self.offsets]
        for peer in peers:
            pl.semaphore_signal(
                barrier, inc=1, device_id=self.device(peer), device_id_type=pl.DeviceIdType.MESH
            )

    def admit(self):
        pl.semaphore_wait(pltpu.get_barrier_semaphore(), self.count - 1)

    def put(self, source, target, peer, send_sem, recv_sem):
        pltpu.make_async_remote_copy(
            src_ref=source,
            dst_ref=target,
            send_sem=send_sem,
            recv_sem=recv_sem,
            device_id=self.device(peer),
            device_id_type=pl.DeviceIdType.MESH,
        ).start()


def await_bytes(ref, sem):
    pltpu.make_async_copy(ref, ref, sem).wait()


def layer_kernel(
    shape, n_time, frame_group,
    vis_ref, tok_ref, attn_ref, in_hbm, out_hbm, virt_hbm, virtual_ref, dest_ref,
    time_ones, sort_ref, side_ref, home_ref, query_ref, in_ref, out_ref, virt_ref,
    slab, inbox, extra, x_ref, key_ref, value_ref, qb_ref, hub_ref, outbox,
    in_sem, out_sem, weight_sem, send1, recv1, local1, send_extra, recv_extra, local_extra,
    send_hub, recv_hub, send2, recv2, local2,
):
    step = pl.program_id(0)
    group, frames, feature = tok_ref.shape
    n_virtual = virtual_ref.shape[0]
    exchange = Exchange(shape)
    count, side = exchange.count, exchange.side
    local, here, there = exchange.local, exchange.here, exchange.there
    each = frames // count
    side_chunk = side * group
    own_tracks = n_time * group
    side_tracks = side * own_tracks
    lag = n_time - 3
    n_whole = n_time - DEFER
    short = each // 2
    pair = 2 * side_chunk

    @pl.when(step == 0)
    def _():
        pltpu.make_async_copy(in_hbm, in_ref, in_sem).start()
        pltpu.make_async_copy(out_hbm, out_ref, out_sem).start()
        exchange.greet()
        pltpu.make_async_copy(virt_hbm, virt_ref, weight_sem).start()
        fill_ones(time_ones, feature)

    def share(half, index):
        slot = half * n_time + index
        for j in range(side):
            peer = there + exchange.near(j)
            exchange.put(
                slab.at[half, index, peer], inbox.at[half, index, side + local], peer, send1, recv1.at[slot]
            )
        for j in exchange.offsets:
            peer = here + exchange.near(j)
            exchange.put(slab.at[half, index, peer], inbox.at[half, index, local], peer, send1, recv1.at[slot])
        for j in exchange.offsets:
            near = exchange.near(j)
            exchange.put(
                slab.at[half, index, there + near], extra.at[half, index, local], here + near,
                send_extra, recv_extra.at[slot],
            )
        pltpu.make_async_copy(
            slab.at[half, index, here + local], inbox.at[half, index, local], local1.at[slot]
        ).start()
        pltpu.make_async_copy(
            slab.at[half, index, there + local], extra.at[half, index, local], local_extra.at[slot]
        ).start()

    def ready():
        @pl.when(step == 0)
        def _():
            pltpu.make_async_copy(in_hbm, in_ref, in_sem).wait()
            pltpu.make_async_copy(out_hbm, out_ref, out_sem).wait()

    @pl.when(step < n_time)
    def _():
        begin = [vis_ref[0, step * group + i] for i in range(group)]
        end = [vis_ref[1, step * group + i] for i in range(group)]
        after = time_step(tok_ref[...], begin, end, attn_ref, in_ref, out_ref, time_ones, ready)
        for half, block in enumerate(interleave(after[:frames], after[frames:], count)):
            slab[half, step] = block.astype(BF16)

        @pl.when(step == 0)
        def _():
            exchange.admit()

        share(0, step)

        @pl.when(step < n_whole)
        def _():
            share(1, step)

        @pl.when(step == n_time - 1)
        def _():
            for index in range(n_whole, n_time):
                share(1, index)

    @pl.when(step == lag)
    def _():
        pltpu.make_async_copy(virt_hbm, virt_ref, weight_sem).wait()
        query = project(layer_norm(virtual_ref[...]), virt_ref[0, 0]).astype(BF16)
        for at, heads in enumerate(head_groups(feature)):
            query_ref[at] = spread_heads(query, head_masks(feature, BF16), heads)
        for ref, sides in ((sort_ref, 2), (side_ref, 1)):
            row = lax.broadcasted_iota(jnp.int32, ref.shape, 0)
            col = lax.broadcasted_iota(jnp.int32, ref.shape, 1)
            frame, track = row // (sides * pair), row % (sides * pair)
            far, track = track // pair, track % pair
            index, track = track // side_chunk, track % side_chunk
            sender = index * sides * side + far * side + track // group
            place = sender * each + track % group * short + frame
            ref[...] = jnp.where(col == place, 1.0, 0.0).astype(BF16)
        row = lax.broadcasted_iota(jnp.int32, home_ref.shape, 0)
        col = lax.broadcasted_iota(jnp.int32, home_ref.shape, 1)
        track = row % own_tracks
        place = track // group * side_chunk + row // own_tracks * group + track % group
        home_ref[...] = jnp.where(col == place, 1.0, 0.0).astype(BF16)

    def arrive(half, couple):
        whole, second = [], []
        for i in range(2):
            index = 2 * couple + i
            slot = half * n_time + index
            await_bytes(inbox.at[half, index, pl.ds(0, count - 1)], recv1.at[slot])
            await_bytes(inbox.at[half, index, 0], local1.at[slot])
            await_bytes(extra.at[half, index, pl.ds(0, side - 1)], recv_extra.at[slot])
            await_bytes(extra.at[half, index, 0], local_extra.at[slot])
        steps = slice(2 * couple, 2 * couple + 2)
        whole = project(sort_ref[...], inbox[half, steps].reshape(2 * count * each, feature)).astype(BF16)
        second = project(side_ref[...], extra[half, steps].reshape(2 * side * each, feature)).astype(BF16)
        normed = layer_norm(whole)
        second_normed = layer_norm(second).reshape(short, pair, feature)
        second = second.reshape(short, pair, feature)
        span = slice(half * short, (half + 1) * short)
        far_span = slice(each + half * short, each + (half + 1) * short)
        place = slice(2 * pair * couple, 2 * pair * (couple + 1))
        key_ref[span, place] = project(normed, virt_ref[0, 1]).astype(BF16).reshape(short, 2 * pair, feature)
        value_ref[span, place] = project(normed, virt_ref[0, 2]).astype(BF16).reshape(short, 2 * pair, feature)
        mine = whole.reshape(short, 2 * pair, feature)[:, :pair]
        mine_normed = normed.reshape(short, 2 * pair, feature)[:, :pair]
        both = jnp.concatenate([mine_normed, second_normed], axis=0).reshape(2 * short * pair, feature)
        query = project(both, virt_ref[2, 0]).astype(BF16).reshape(2 * short, pair, feature)
        place = slice(pair * couple, pair * (couple + 1))
        x_ref[span, place] = mine
        x_ref[far_span, place] = second
        qb_ref[span, place] = query[:short]
        qb_ref[far_span, place] = query[short:]

    def make_hub(part):
        span = pl.ds(part * frame_group, frame_group)
        hub_ref[0, part] = virtual_step(key_ref[span], value_ref[span], virt_ref, virtual_ref, query_ref)
        exchange.put(
            hub_ref.at[0, part], hub_ref.at[1, part], there + local, send_hub, recv_hub.at[part]
        )

    def give_back(which, part):
        first = which * each + part * frame_group
        span = pl.ds(first, frame_group)
        after = back_step(x_ref[span], qb_ref[span], hub_ref[which, part], virt_ref).astype(BF16)
        for f in range(frame_group):
            block = project(home_ref[...], after[f * side_tracks : (f + 1) * side_tracks]).astype(BF16)
            outbox[:, first + f] = block.reshape(side, own_tracks, feature)
        owner = (here if which == 0 else there) + local
        target = dest_ref.at[pl.ds(owner * each + part * frame_group, frame_group)]
        for j in exchange.offsets:
            near = exchange.near(j)
            exchange.put(outbox.at[near, span], target, here + near, send2, recv2)
        pltpu.make_async_copy(outbox.at[local, span], target, local2).start()

    for at, jobs in enumerate(PLAN):
        @pl.when(step == at)
        def _(jobs=jobs):
            for kind, which, part in jobs:
                if kind == "arrive":
                    arrive(which, part)
                elif kind == "hub":
                    make_hub(part)
                else:
                    if which == 1:
                        await_bytes(hub_ref.at[1, part], recv_hub.at[part])
                    give_back(which, part)

    @pl.when(step == pl.num_programs(0) - 1)
    def _():
        await_bytes(slab.at[:, :, pl.ds(0, count - 1)], send1)
        await_bytes(slab.at[:, :, pl.ds(0, side - 1)], send_extra)
        await_bytes(hub_ref.at[0], send_hub)
        others = dest_ref.at[pl.ds(0, (side - 1) * 2 * each)]
        await_bytes(dest_ref.at[pl.ds(0, 2 * each)], local2)
        await_bytes(others, send2)
        await_bytes(others, recv2)


WHOLE = pl.BlockSpec(memory_space=pltpu.VMEM)
ANY = pl.BlockSpec(memory_space=pl.ANY)
DEFER = 0
GROUP = 4
PLAN = (
    [],
    [],
    [],
    [],
    [],
    [],
    [],
    [("arrive", 0, 0)],
    [("arrive", 1, 0)],
    [("arrive", 0, 1)],
    [("arrive", 1, 1)],
    [("arrive", 0, 2)],
    [("arrive", 1, 2)],
    [("arrive", 0, 3)],
    [("hub", 0, 0)],
    [("arrive", 1, 3), ("back", 0, 0)],
    [("hub", 0, 1)],
    [("back", 0, 1)],
    [("back", 1, 0)],
    [("back", 1, 1)],
)
LIMIT = 60 * 1024 * 1024


def shards(shape, tokens, visible, time_attn, mlp_in, mlp_out, virt_attn, virtual):
    own_tracks, frames, feature = tokens.shape
    n_virtual = virtual.shape[0]
    count = shape["track"] * shape["sub"]
    side = count // 2
    each = frames // count
    group, frame_group = 2, GROUP
    n_time = own_tracks // group
    parts = each // frame_group
    dma = pltpu.SemaphoreType.DMA
    window = head_groups(feature)[0][1].stop
    result = pl.pallas_call(
        functools.partial(layer_kernel, shape, n_time, frame_group),
        grid=(len(PLAN),),
        in_specs=[
            pl.BlockSpec(memory_space=pltpu.SMEM),
            pl.BlockSpec((group, frames, feature), lambda i: (jnp.minimum(i, n_time - 1), 0, 0)),
            WHOLE, ANY, ANY, ANY, WHOLE,
        ],
        out_specs=ANY,
        out_shape=jax.ShapeDtypeStruct((frames, own_tracks, feature), BF16),
        scratch_shapes=[
            pltpu.VMEM((2, HEADS // 2 * frames, window), BF16),
            pltpu.VMEM((count * group * each, count * group * each), BF16),
            pltpu.VMEM((side * group * each, side * group * each), BF16),
            pltpu.VMEM((side * own_tracks, side * own_tracks), BF16),
            pltpu.VMEM((2, HEADS // 2 * n_virtual, window), BF16),
            pltpu.VMEM(mlp_in.shape, BF16),
            pltpu.VMEM(mlp_out.shape, BF16),
            pltpu.VMEM(virt_attn.shape, BF16),
            pltpu.VMEM((2, n_time, count, each, feature), BF16),
            pltpu.VMEM((2, n_time, count, each, feature), BF16),
            pltpu.VMEM((2, n_time, side, each, feature), BF16),
            pltpu.VMEM((2 * each, side * own_tracks, feature), BF16),
            pltpu.VMEM((each, count * own_tracks, feature), BF16),
            pltpu.VMEM((each, count * own_tracks, feature), BF16),
            pltpu.VMEM((2 * each, side * own_tracks, feature), BF16),
            pltpu.VMEM((2, parts, frame_group * n_virtual, feature), BF16),
            pltpu.VMEM((side, 2 * each, own_tracks, feature), BF16),
            dma, dma, dma,
            dma, dma((2 * n_time,)), dma((2 * n_time,)),
            dma, dma((2 * n_time,)), dma((2 * n_time,)),
            dma, dma((parts,)),
            dma, dma, dma,
        ],
        compiler_params=pltpu.CompilerParams(vmem_limit_bytes=LIMIT, collective_id=0, has_side_effects=True),
    )(visible.T, tokens, time_attn, mlp_in, mlp_out, virt_attn, virtual)
    return jnp.swapaxes(result, 0, 1)


def solution(mesh):
    placed = (
        P(("groups", "track", "sub"), None, None),
        P(("groups", "track", "sub"), None),
        P(),
        P(),
        P(),
        P(),
        P(),
    )
    return jax.shard_map(
        functools.partial(shards, dict(mesh.shape)),
        mesh=mesh,
        in_specs=placed,
        out_specs=P(("groups", "track", "sub"), None, None),
        check_vma=False,
    )
```

```python
import functools
import math

import jax
import jax.numpy as jnp
from jax import lax
from jax.experimental import pallas as pl
from jax.experimental.pallas import tpu as pltpu
from jax.sharding import PartitionSpec as P

HEADS = 8
LANES = 128
LOG2E = math.log2(math.e)
F32 = jnp.float32
BF16 = jnp.bfloat16


def layer_norm(values):
    wide = values.astype(F32)
    center = wide - jnp.mean(wide, axis=-1, keepdims=True)
    spread = jnp.mean(center * center, axis=-1, keepdims=True)
    return (center * lax.rsqrt(spread + 1e-05)).astype(BF16)


def project(values, matrix):
    return jnp.dot(values, matrix, preferred_element_type=F32)


def product(left, right, left_dim, right_dim):
    dims = (((left_dim,), (right_dim,)), ((), ()))
    return lax.dot_general(left, right, dims, preferred_element_type=F32)


def head_masks(feature, kind):
    size = feature // HEADS
    lanes = lax.broadcasted_iota(jnp.int32, (1, feature), 1)
    return [
        jnp.where((lanes >= head * size) & (lanes < (head + 1) * size), 1.0, 0.0).astype(kind)
        for head in range(HEADS)
    ]


def head_groups(feature):
    middle = feature // 2
    heads = HEADS // 2
    return (
        (range(heads), slice(0, -(-middle // LANES) * LANES)),
        (range(heads, HEADS), slice(middle // LANES * LANES, feature)),
    )


def spread_heads(rows, masks, group):
    heads, lanes = group
    return jnp.concatenate([rows[:, lanes] * masks[head][:, lanes] for head in heads], axis=0)


def join_groups(low, high, feature):
    (_, first), (_, second) = head_groups(feature)
    shared = first.stop - second.start
    if not shared:
        return jnp.concatenate([low, high], axis=1)
    middle = low[:, second.start :] + high[:, :shared]
    return jnp.concatenate([low[:, : second.start], middle, high[:, shared:]], axis=1)


def time_step(tokens, first_frame, end_frame, attn_ref, in_ref, out_ref, ones_ref, ready):
    tracks, frames, feature = tokens.shape
    scale = LOG2E / math.sqrt(feature // HEADS)
    groups = head_groups(feature)
    masks = head_masks(feature, BF16)
    wide = tokens.reshape(tracks * frames, feature).astype(F32)
    normed = layer_norm(wide)
    queries = project(normed, attn_ref[0]).astype(BF16)
    keys = project(normed, attn_ref[1]).astype(BF16)
    values = project(normed, attn_ref[2]).astype(BF16)
    lane = lax.broadcasted_iota(jnp.int32, (1, frames), 1)
    row = lax.broadcasted_iota(jnp.int32, (frames, feature), 0)
    mixed, vis = [], []
    for track in range(tracks):
        part = slice(track * frames, (track + 1) * frames)
        seen = (lane >= first_frame[track]) & (lane < end_frame[track])
        outs = []
        for at, group in enumerate(groups):
            heads, lanes = group
            scores = product(queries[part, lanes], spread_heads(keys[part], masks, group), 1, 1)
            weights = []
            for head in range(len(heads)):
                own = scores[:, head * frames : (head + 1) * frames]
                own = jnp.where(seen, own, -1e30)
                top = jnp.max(own, axis=-1, keepdims=True)
                weights.append(jnp.exp2((own - top) * scale).astype(BF16))
            weights = jnp.concatenate(weights, axis=1)
            outs.append(project(weights, spread_heads(values[part], masks, group)))
            outs.append(project(weights, ones_ref[at]))
        summed = join_groups(outs[0], outs[2], feature)
        total = join_groups(outs[1], outs[3], feature)
        mixed.append((summed / total).astype(BF16))
        shown = (row >= first_frame[track]) & (row < end_frame[track])
        vis.append(jnp.where(shown, 1.0, 0.0).astype(F32))
    mixed = jnp.concatenate(mixed, axis=0)
    vis = jnp.concatenate(vis, axis=0)
    first = wide + vis * project(mixed, attn_ref[3])
    ready()
    hidden = jax.nn.gelu(project(layer_norm(first), in_ref[...]), approximate=True).astype(BF16)
    return first + vis * project(hidden, out_ref[...])


def fill_ones(ones_ref, feature):
    rows = ones_ref.shape[1] // (HEADS // 2)
    masks = head_masks(feature, F32)
    for at, (heads, lanes) in enumerate(head_groups(feature)):
        for place, head in enumerate(heads):
            mask = masks[head][:, lanes]
            ones_ref[at, place * rows : (place + 1) * rows, :] = jnp.broadcast_to(
                mask, (rows, mask.shape[1])
            ).astype(BF16)


def few_queries(spread_queries, keys, values, wide_masks):
    feature = keys.shape[1]
    scale = LOG2E / math.sqrt(feature // HEADS)
    outs = []
    for queries, (heads, lanes) in zip(spread_queries, head_groups(feature)):
        scores = product(queries, keys[:, lanes], 1, 1)
        top = jnp.max(scores, axis=-1, keepdims=True)
        weights = jnp.exp2((scores - top) * scale)
        total = jnp.sum(weights, axis=-1, keepdims=True)
        summed = project(weights.astype(BF16), values[:, lanes]) * (1.0 / total)
        count = queries.shape[0] // len(heads)
        mixed = 0.0
        for place, head in enumerate(heads):
            mixed = mixed + summed[place * count : (place + 1) * count] * wide_masks[head][:, lanes]
        outs.append(mixed)
    return join_groups(outs[0], outs[1], feature).astype(BF16)


def virtual_step(key_c, value_c, attn_ref, virtual_ref, query_ref):
    frames, tracks, feature = key_c.shape
    n_virtual = virtual_ref.shape[0]
    masks = head_masks(feature, BF16)
    wide_masks = head_masks(feature, F32)
    groups = head_groups(feature)
    virtual_part = [slice(f * n_virtual, (f + 1) * n_virtual) for f in range(frames)]
    cross = [few_queries((query_ref[0], query_ref[1]), key_c[f], value_c[f], wide_masks) for f in range(frames)]
    base = jnp.concatenate([virtual_ref[...].astype(F32)] * frames, axis=0)
    first = base + project(jnp.concatenate(cross, axis=0), attn_ref[0, 3])
    normed_w = layer_norm(first)
    query_s = project(normed_w, attn_ref[1, 0]).astype(BF16)
    key_s = project(normed_w, attn_ref[1, 1]).astype(BF16)
    value_s = project(normed_w, attn_ref[1, 2]).astype(BF16)
    among = [
        few_queries([spread_heads(query_s[part], masks, group) for group in groups], key_s[part], value_s[part], wide_masks)
        for part in virtual_part
    ]
    second = first + project(jnp.concatenate(among, axis=0), attn_ref[1, 3])
    return layer_norm(second)


def back_step(wide, query_b, normed_b, attn_ref, ones_ref):
    frames, tracks, feature = wide.shape
    n_virtual = normed_b.shape[0] // frames
    scale = LOG2E / math.sqrt(feature // HEADS)
    masks = head_masks(feature, BF16)
    wide = wide.reshape(frames * tracks, feature).astype(F32)
    key_b = project(normed_b, attn_ref[2, 1]).astype(BF16)
    value_b = project(normed_b, attn_ref[2, 2]).astype(BF16)
    back = []
    for frame in range(frames):
        part = slice(frame * n_virtual, (frame + 1) * n_virtual)
        outs = []
        for at, group in enumerate(head_groups(feature)):
            heads, lanes = group
            scores = product(spread_heads(key_b[part], masks, group), query_b[frame][:, lanes], 1, 1)
            scores = scores.reshape(len(heads), n_virtual, tracks)
            top = jnp.max(scores, axis=1, keepdims=True)
            weights = jnp.exp2((scores - top) * scale)
            weights = weights.astype(BF16).reshape(len(heads) * n_virtual, tracks)
            outs.append(product(weights, spread_heads(value_b[part], masks, group), 0, 0))
            outs.append(product(weights, ones_ref[at], 0, 0))
        summed = join_groups(outs[0], outs[2], feature)
        back.append((summed / join_groups(outs[1], outs[3], feature)).astype(BF16))
    return wide + project(jnp.concatenate(back, axis=0), attn_ref[2, 3])


def interleave(first, second, count):
    frames, feature = first.shape
    each = frames // count
    first = first.reshape(count, each, feature)
    second = second.reshape(count, each, feature)
    row = lax.broadcasted_iota(jnp.int32, first.shape, 1)
    short = each // 2
    early = jnp.where(row < short, first, pltpu.roll(second, short, 1))
    late = jnp.where(row < short, pltpu.roll(first, short, 1), second)
    return early, late


class Exchange:
    def __init__(self, shape):
        self.n_sub = shape["sub"]
        self.count = shape["track"] * shape["sub"]
        self.side = self.count // 2
        me = lax.axis_index("track") * self.n_sub + lax.axis_index("sub")
        self.local = lax.rem(me, self.side)
        self.here = me - self.local
        self.there = self.side - self.here
        self.offsets = sorted(range(1, self.side), key=lambda j: abs(2 * j - self.side))

    def near(self, offset):
        return lax.rem(self.local + offset, self.side)

    def device(self, peer):
        return {"track": peer // self.n_sub, "sub": peer % self.n_sub}

    def greet(self):
        barrier = pltpu.get_barrier_semaphore()
        peers = [self.there + self.near(j) for j in range(self.side)]
        peers += [self.here + self.near(j) for j in self.offsets]
        for peer in peers:
            pl.semaphore_signal(
                barrier, inc=1, device_id=self.device(peer), device_id_type=pl.DeviceIdType.MESH
            )

    def admit(self):
        pl.semaphore_wait(pltpu.get_barrier_semaphore(), self.count - 1)

    def put(self, source, target, peer, send_sem, recv_sem):
        pltpu.make_async_remote_copy(
            src_ref=source,
            dst_ref=target,
            send_sem=send_sem,
            recv_sem=recv_sem,
            device_id=self.device(peer),
            device_id_type=pl.DeviceIdType.MESH,
        ).start()


def await_bytes(ref, sem):
    pltpu.make_async_copy(ref, ref, sem).wait()


def layer_kernel(
    shape, n_time, frame_group,
    vis_ref, tok_ref, attn_ref, in_hbm, out_hbm, virt_hbm, virtual_ref, dest_ref,
    time_ones, frame_ones, sort_ref, side_ref, home_ref, query_ref, in_ref, out_ref, virt_ref,
    slab, inbox, extra, x_ref, key_ref, value_ref, qb_ref, hub_ref, outbox,
    in_sem, out_sem, weight_sem, send1, recv1, local1, send_extra, recv_extra, local_extra,
    send_hub, recv_hub, send2, recv2, local2,
):
    step = pl.program_id(0)
    group, frames, feature = tok_ref.shape
    n_virtual = virtual_ref.shape[0]
    exchange = Exchange(shape)
    count, side = exchange.count, exchange.side
    local, here, there = exchange.local, exchange.here, exchange.there
    each = frames // count
    side_chunk = side * group
    own_tracks = n_time * group
    side_tracks = side * own_tracks
    lag = n_time - 3
    n_whole = n_time - DEFER
    short = each // 2
    pair = 2 * side_chunk

    @pl.when(step == 0)
    def _():
        pltpu.make_async_copy(in_hbm, in_ref, in_sem).start()
        pltpu.make_async_copy(out_hbm, out_ref, out_sem).start()
        exchange.greet()
        pltpu.make_async_copy(virt_hbm, virt_ref, weight_sem).start()
        fill_ones(time_ones, feature)

    def share(half, index):
        slot = half * n_time + index
        for j in range(side):
            peer = there + exchange.near(j)
            exchange.put(
                slab.at[half, index, peer], inbox.at[half, index, side + local], peer, send1, recv1.at[slot]
            )
        for j in exchange.offsets:
            peer = here + exchange.near(j)
            exchange.put(slab.at[half, index, peer], inbox.at[half, index, local], peer, send1, recv1.at[slot])
        for j in exchange.offsets:
            near = exchange.near(j)
            exchange.put(
                slab.at[half, index, there + near], extra.at[half, index, local], here + near,
                send_extra, recv_extra.at[slot],
            )
        pltpu.make_async_copy(
            slab.at[half, index, here + local], inbox.at[half, index, local], local1.at[slot]
        ).start()
        pltpu.make_async_copy(
            slab.at[half, index, there + local], extra.at[half, index, local], local_extra.at[slot]
        ).start()

    def ready():
        @pl.when(step == 0)
        def _():
            pltpu.make_async_copy(in_hbm, in_ref, in_sem).wait()
            pltpu.make_async_copy(out_hbm, out_ref, out_sem).wait()

    @pl.when(step < n_time)
    def _():
        begin = [vis_ref[0, step * group + i] for i in range(group)]
        end = [vis_ref[1, step * group + i] for i in range(group)]
        after = time_step(tok_ref[...], begin, end, attn_ref, in_ref, out_ref, time_ones, ready)
        for half, block in enumerate(interleave(after[:frames], after[frames:], count)):
            slab[half, step] = block.astype(BF16)

        @pl.when(step == 0)
        def _():
            exchange.admit()

        share(0, step)

        @pl.when(step < n_whole)
        def _():
            share(1, step)

        @pl.when(step == n_time - 1)
        def _():
            for index in range(n_whole, n_time):
                share(1, index)

    @pl.when(step == lag)
    def _():
        pltpu.make_async_copy(virt_hbm, virt_ref, weight_sem).wait()
        query = project(layer_norm(virtual_ref[...]), virt_ref[0, 0]).astype(BF16)
        fill_ones(frame_ones, feature)
        for at, heads in enumerate(head_groups(feature)):
            query_ref[at] = spread_heads(query, head_masks(feature, BF16), heads)
        for ref, sides in ((sort_ref, 2), (side_ref, 1)):
            row = lax.broadcasted_iota(jnp.int32, ref.shape, 0)
            col = lax.broadcasted_iota(jnp.int32, ref.shape, 1)
            frame, track = row // (sides * pair), row % (sides * pair)
            far, track = track // pair, track % pair
            index, track = track // side_chunk, track % side_chunk
            sender = index * sides * side + far * side + track // group
            place = sender * each + track % group * short + frame
            ref[...] = jnp.where(col == place, 1.0, 0.0).astype(BF16)
        row = lax.broadcasted_iota(jnp.int32, home_ref.shape, 0)
        col = lax.broadcasted_iota(jnp.int32, home_ref.shape, 1)
        track = row % own_tracks
        place = track // group * side_chunk + row // own_tracks * group + track % group
        home_ref[...] = jnp.where(col == place, 1.0, 0.0).astype(BF16)

    def arrive(half, couple):
        whole, second = [], []
        for i in range(2):
            index = 2 * couple + i
            slot = half * n_time + index
            await_bytes(inbox.at[half, index, pl.ds(0, count - 1)], recv1.at[slot])
            await_bytes(inbox.at[half, index, 0], local1.at[slot])
            await_bytes(extra.at[half, index, pl.ds(0, side - 1)], recv_extra.at[slot])
            await_bytes(extra.at[half, index, 0], local_extra.at[slot])
        steps = slice(2 * couple, 2 * couple + 2)
        whole = project(sort_ref[...], inbox[half, steps].reshape(2 * count * each, feature)).astype(BF16)
        second = project(side_ref[...], extra[half, steps].reshape(2 * side * each, feature)).astype(BF16)
        normed = layer_norm(whole)
        second_normed = layer_norm(second).reshape(short, pair, feature)
        second = second.reshape(short, pair, feature)
        span = slice(half * short, (half + 1) * short)
        far_span = slice(each + half * short, each + (half + 1) * short)
        place = slice(2 * pair * couple, 2 * pair * (couple + 1))
        key_ref[span, place] = project(normed, virt_ref[0, 1]).astype(BF16).reshape(short, 2 * pair, feature)
        value_ref[span, place] = project(normed, virt_ref[0, 2]).astype(BF16).reshape(short, 2 * pair, feature)
        mine = whole.reshape(short, 2 * pair, feature)[:, :pair]
        mine_normed = normed.reshape(short, 2 * pair, feature)[:, :pair]
        both = jnp.concatenate([mine_normed, second_normed], axis=0).reshape(2 * short * pair, feature)
        query = project(both, virt_ref[2, 0]).astype(BF16).reshape(2 * short, pair, feature)
        place = slice(pair * couple, pair * (couple + 1))
        x_ref[span, place] = mine
        x_ref[far_span, place] = second
        qb_ref[span, place] = query[:short]
        qb_ref[far_span, place] = query[short:]

    def make_hub(part):
        span = pl.ds(part * frame_group, frame_group)
        hub_ref[0, part] = virtual_step(key_ref[span], value_ref[span], virt_ref, virtual_ref, query_ref)
        exchange.put(
            hub_ref.at[0, part], hub_ref.at[1, part], there + local, send_hub, recv_hub.at[part]
        )

    def give_back(which, part):
        first = which * each + part * frame_group
        span = pl.ds(first, frame_group)
        after = back_step(x_ref[span], qb_ref[span], hub_ref[which, part], virt_ref, frame_ones).astype(BF16)
        for f in range(frame_group):
            block = project(home_ref[...], after[f * side_tracks : (f + 1) * side_tracks]).astype(BF16)
            outbox[:, first + f] = block.reshape(side, own_tracks, feature)
        owner = (here if which == 0 else there) + local
        target = dest_ref.at[pl.ds(owner * each + part * frame_group, frame_group)]
        for j in exchange.offsets:
            near = exchange.near(j)
            exchange.put(outbox.at[near, span], target, here + near, send2, recv2)
        pltpu.make_async_copy(outbox.at[local, span], target, local2).start()

    for at, jobs in enumerate(PLAN):
        @pl.when(step == at)
        def _(jobs=jobs):
            for kind, which, part in jobs:
                if kind == "arrive":
                    arrive(which, part)
                elif kind == "hub":
                    make_hub(part)
                else:
                    if which == 1:
                        await_bytes(hub_ref.at[1, part], recv_hub.at[part])
                    give_back(which, part)

    @pl.when(step == pl.num_programs(0) - 1)
    def _():
        await_bytes(slab.at[:, :, pl.ds(0, count - 1)], send1)
        await_bytes(slab.at[:, :, pl.ds(0, side - 1)], send_extra)
        await_bytes(hub_ref.at[0], send_hub)
        others = dest_ref.at[pl.ds(0, (side - 1) * 2 * each)]
        await_bytes(dest_ref.at[pl.ds(0, 2 * each)], local2)
        await_bytes(others, send2)
        await_bytes(others, recv2)


WHOLE = pl.BlockSpec(memory_space=pltpu.VMEM)
ANY = pl.BlockSpec(memory_space=pl.ANY)
DEFER = 0
GROUP = 4
PLAN = (
    [],
    [],
    [],
    [],
    [],
    [],
    [],
    [("arrive", 0, 0)],
    [("arrive", 1, 0)],
    [("arrive", 0, 1)],
    [("arrive", 1, 1)],
    [("arrive", 0, 2)],
    [("arrive", 1, 2)],
    [("arrive", 0, 3)],
    [("hub", 0, 0)],
    [("back", 0, 0)],
    [("arrive", 1, 3)],
    [("hub", 0, 1)],
    [("back", 1, 0)],
    [("back", 0, 1)],
    [("back", 1, 1)],
)
LIMIT = 60 * 1024 * 1024


def shards(shape, tokens, visible, time_attn, mlp_in, mlp_out, virt_attn, virtual):
    own_tracks, frames, feature = tokens.shape
    n_virtual = virtual.shape[0]
    count = shape["track"] * shape["sub"]
    side = count // 2
    each = frames // count
    group, frame_group = 2, GROUP
    n_time = own_tracks // group
    parts = each // frame_group
    dma = pltpu.SemaphoreType.DMA
    window = head_groups(feature)[0][1].stop
    result = pl.pallas_call(
        functools.partial(layer_kernel, shape, n_time, frame_group),
        grid=(len(PLAN),),
        in_specs=[
            pl.BlockSpec(memory_space=pltpu.SMEM),
            pl.BlockSpec((group, frames, feature), lambda i: (jnp.minimum(i, n_time - 1), 0, 0)),
            WHOLE, ANY, ANY, ANY, WHOLE,
        ],
        out_specs=ANY,
        out_shape=jax.ShapeDtypeStruct((frames, own_tracks, feature), BF16),
        scratch_shapes=[
            pltpu.VMEM((2, HEADS // 2 * frames, window), BF16),
            pltpu.VMEM((2, HEADS // 2 * n_virtual, window), BF16),
            pltpu.VMEM((count * group * each, count * group * each), BF16),
            pltpu.VMEM((side * group * each, side * group * each), BF16),
            pltpu.VMEM((side * own_tracks, side * own_tracks), BF16),
            pltpu.VMEM((2, HEADS // 2 * n_virtual, window), BF16),
            pltpu.VMEM(mlp_in.shape, BF16),
            pltpu.VMEM(mlp_out.shape, BF16),
            pltpu.VMEM(virt_attn.shape, BF16),
            pltpu.VMEM((2, n_time, count, each, feature), BF16),
            pltpu.VMEM((2, n_time, count, each, feature), BF16),
            pltpu.VMEM((2, n_time, side, each, feature), BF16),
            pltpu.VMEM((2 * each, side * own_tracks, feature), BF16),
            pltpu.VMEM((each, count * own_tracks, feature), BF16),
            pltpu.VMEM((each, count * own_tracks, feature), BF16),
            pltpu.VMEM((2 * each, side * own_tracks, feature), BF16),
            pltpu.VMEM((2, parts, frame_group * n_virtual, feature), BF16),
            pltpu.VMEM((side, 2 * each, own_tracks, feature), BF16),
            dma, dma, dma,
            dma, dma((2 * n_time,)), dma((2 * n_time,)),
            dma, dma((2 * n_time,)), dma((2 * n_time,)),
            dma, dma((parts,)),
            dma, dma, dma,
        ],
        compiler_params=pltpu.CompilerParams(vmem_limit_bytes=LIMIT, collective_id=0, has_side_effects=True),
    )(visible.T, tokens, time_attn, mlp_in, mlp_out, virt_attn, virtual)
    return jnp.swapaxes(result, 0, 1)


def solution(mesh):
    placed = (
        P(("groups", "track", "sub"), None, None),
        P(("groups", "track", "sub"), None),
        P(),
        P(),
        P(),
        P(),
        P(),
    )
    return jax.shard_map(
        functools.partial(shards, dict(mesh.shape)),
        mesh=mesh,
        in_specs=placed,
        out_specs=P(("groups", "track", "sub"), None, None),
        check_vma=False,
    )
```

```python
import functools
import math

import jax
import jax.numpy as jnp
from jax import lax
from jax.experimental import pallas as pl
from jax.experimental.pallas import tpu as pltpu
from jax.sharding import PartitionSpec as P

HEADS = 8
LANES = 128
LOG2E = math.log2(math.e)
F32 = jnp.float32
BF16 = jnp.bfloat16


def layer_norm(values):
    wide = values.astype(F32)
    center = wide - jnp.mean(wide, axis=-1, keepdims=True)
    spread = jnp.mean(center * center, axis=-1, keepdims=True)
    return (center * lax.rsqrt(spread + 1e-05)).astype(BF16)


def project(values, matrix):
    return jnp.dot(values, matrix, preferred_element_type=F32)


def product(left, right, left_dim, right_dim):
    dims = (((left_dim,), (right_dim,)), ((), ()))
    return lax.dot_general(left, right, dims, preferred_element_type=F32)


def head_masks(feature, kind):
    size = feature // HEADS
    lanes = lax.broadcasted_iota(jnp.int32, (1, feature), 1)
    return [
        jnp.where((lanes >= head * size) & (lanes < (head + 1) * size), 1.0, 0.0).astype(kind)
        for head in range(HEADS)
    ]


def head_groups(feature):
    middle = feature // 2
    heads = HEADS // 2
    return (
        (range(heads), slice(0, -(-middle // LANES) * LANES)),
        (range(heads, HEADS), slice(middle // LANES * LANES, feature)),
    )


def spread_heads(rows, masks, group):
    heads, lanes = group
    return jnp.concatenate([rows[:, lanes] * masks[head][:, lanes] for head in heads], axis=0)


def join_groups(low, high, feature):
    (_, first), (_, second) = head_groups(feature)
    shared = first.stop - second.start
    if not shared:
        return jnp.concatenate([low, high], axis=1)
    middle = low[:, second.start :] + high[:, :shared]
    return jnp.concatenate([low[:, : second.start], middle, high[:, shared:]], axis=1)


def time_step(tokens, first_frame, end_frame, attn_ref, in_ref, out_ref, ones_ref, ready):
    tracks, frames, feature = tokens.shape
    scale = LOG2E / math.sqrt(feature // HEADS)
    groups = head_groups(feature)
    masks = head_masks(feature, BF16)
    wide = tokens.reshape(tracks * frames, feature).astype(F32)
    normed = layer_norm(wide)
    queries = project(normed, attn_ref[0]).astype(BF16)
    keys = project(normed, attn_ref[1]).astype(BF16)
    values = project(normed, attn_ref[2]).astype(BF16)
    lane = lax.broadcasted_iota(jnp.int32, (1, frames), 1)
    row = lax.broadcasted_iota(jnp.int32, (frames, feature), 0)
    mixed, vis = [], []
    for track in range(tracks):
        part = slice(track * frames, (track + 1) * frames)
        seen = (lane >= first_frame[track]) & (lane < end_frame[track])
        outs = []
        for at, group in enumerate(groups):
            heads, lanes = group
            scores = product(queries[part, lanes], spread_heads(keys[part], masks, group), 1, 1)
            weights = []
            for head in range(len(heads)):
                own = scores[:, head * frames : (head + 1) * frames]
                own = jnp.where(seen, own, -1e30)
                top = jnp.max(own, axis=-1, keepdims=True)
                weights.append(jnp.exp2((own - top) * scale).astype(BF16))
            weights = jnp.concatenate(weights, axis=1)
            outs.append(project(weights, spread_heads(values[part], masks, group)))
            outs.append(project(weights, ones_ref[at]))
        summed = join_groups(outs[0], outs[2], feature)
        total = join_groups(outs[1], outs[3], feature)
        mixed.append((summed / total).astype(BF16))
        shown = (row >= first_frame[track]) & (row < end_frame[track])
        vis.append(jnp.where(shown, 1.0, 0.0).astype(F32))
    mixed = jnp.concatenate(mixed, axis=0)
    vis = jnp.concatenate(vis, axis=0)
    first = wide + vis * project(mixed, attn_ref[3])
    ready()
    hidden = jax.nn.gelu(project(layer_norm(first), in_ref[...]), approximate=True).astype(BF16)
    return first + vis * project(hidden, out_ref[...])


def fill_ones(ones_ref, feature):
    rows = ones_ref.shape[1] // (HEADS // 2)
    masks = head_masks(feature, F32)
    for at, (heads, lanes) in enumerate(head_groups(feature)):
        for place, head in enumerate(heads):
            mask = masks[head][:, lanes]
            ones_ref[at, place * rows : (place + 1) * rows, :] = jnp.broadcast_to(
                mask, (rows, mask.shape[1])
            ).astype(BF16)


def few_queries(spread_queries, keys, values, wide_masks):
    feature = keys.shape[1]
    scale = LOG2E / math.sqrt(feature // HEADS)
    outs = []
    for queries, (heads, lanes) in zip(spread_queries, head_groups(feature)):
        scores = product(queries, keys[:, lanes], 1, 1)
        top = jnp.max(scores, axis=-1, keepdims=True)
        weights = jnp.exp2((scores - top) * scale)
        total = jnp.sum(weights, axis=-1, keepdims=True)
        summed = project(weights.astype(BF16), values[:, lanes]) * (1.0 / total)
        count = queries.shape[0] // len(heads)
        mixed = 0.0
        for place, head in enumerate(heads):
            mixed = mixed + summed[place * count : (place + 1) * count] * wide_masks[head][:, lanes]
        outs.append(mixed)
    return join_groups(outs[0], outs[1], feature).astype(BF16)


def virtual_step(key_c, value_c, attn_ref, virtual_ref, query_ref):
    frames, tracks, feature = key_c.shape
    n_virtual = virtual_ref.shape[0]
    masks = head_masks(feature, BF16)
    wide_masks = head_masks(feature, F32)
    groups = head_groups(feature)
    virtual_part = [slice(f * n_virtual, (f + 1) * n_virtual) for f in range(frames)]
    cross = [few_queries((query_ref[0], query_ref[1]), key_c[f], value_c[f], wide_masks) for f in range(frames)]
    base = jnp.concatenate([virtual_ref[...].astype(F32)] * frames, axis=0)
    first = base + project(jnp.concatenate(cross, axis=0), attn_ref[0, 3])
    normed_w = layer_norm(first)
    query_s = project(normed_w, attn_ref[1, 0]).astype(BF16)
    key_s = project(normed_w, attn_ref[1, 1]).astype(BF16)
    value_s = project(normed_w, attn_ref[1, 2]).astype(BF16)
    among = [
        few_queries([spread_heads(query_s[part], masks, group) for group in groups], key_s[part], value_s[part], wide_masks)
        for part in virtual_part
    ]
    second = first + project(jnp.concatenate(among, axis=0), attn_ref[1, 3])
    return layer_norm(second)


def back_step(wide, query_b, normed_b, attn_ref, ones_ref):
    frames, tracks, feature = wide.shape
    n_virtual = normed_b.shape[0] // frames
    scale = LOG2E / math.sqrt(feature // HEADS)
    masks = head_masks(feature, BF16)
    wide = wide.reshape(frames * tracks, feature).astype(F32)
    key_b = project(normed_b, attn_ref[2, 1]).astype(BF16)
    value_b = project(normed_b, attn_ref[2, 2]).astype(BF16)
    back = []
    for frame in range(frames):
        part = slice(frame * n_virtual, (frame + 1) * n_virtual)
        outs = []
        for at, group in enumerate(head_groups(feature)):
            heads, lanes = group
            scores = product(spread_heads(key_b[part], masks, group), query_b[frame][:, lanes], 1, 1)
            scores = scores.reshape(len(heads), n_virtual, tracks)
            top = jnp.max(scores, axis=1, keepdims=True)
            weights = jnp.exp2((scores - top) * scale)
            weights = weights.astype(BF16).reshape(len(heads) * n_virtual, tracks)
            outs.append(product(weights, spread_heads(value_b[part], masks, group), 0, 0))
            outs.append(product(weights, ones_ref[at], 0, 0))
        summed = join_groups(outs[0], outs[2], feature)
        back.append((summed / join_groups(outs[1], outs[3], feature)).astype(BF16))
    return wide + project(jnp.concatenate(back, axis=0), attn_ref[2, 3])


def interleave(first, second, count):
    frames, feature = first.shape
    each = frames // count
    first = first.reshape(count, each, feature)
    second = second.reshape(count, each, feature)
    row = lax.broadcasted_iota(jnp.int32, first.shape, 1)
    short = each // 2
    early = jnp.where(row < short, first, pltpu.roll(second, short, 1))
    late = jnp.where(row < short, pltpu.roll(first, short, 1), second)
    return early, late


class Exchange:
    def __init__(self, shape):
        self.n_sub = shape["sub"]
        self.count = shape["track"] * shape["sub"]
        self.side = self.count // 2
        me = lax.axis_index("track") * self.n_sub + lax.axis_index("sub")
        self.local = lax.rem(me, self.side)
        self.here = me - self.local
        self.there = self.side - self.here
        self.offsets = sorted(range(1, self.side), key=lambda j: abs(2 * j - self.side))

    def near(self, offset):
        return lax.rem(self.local + offset, self.side)

    def device(self, peer):
        return {"track": peer // self.n_sub, "sub": peer % self.n_sub}

    def greet(self):
        barrier = pltpu.get_barrier_semaphore()
        peers = [self.there + self.near(j) for j in range(self.side)]
        peers += [self.here + self.near(j) for j in self.offsets]
        for peer in peers:
            pl.semaphore_signal(
                barrier, inc=1, device_id=self.device(peer), device_id_type=pl.DeviceIdType.MESH
            )

    def admit(self):
        pl.semaphore_wait(pltpu.get_barrier_semaphore(), self.count - 1)

    def put(self, source, target, peer, send_sem, recv_sem):
        pltpu.make_async_remote_copy(
            src_ref=source,
            dst_ref=target,
            send_sem=send_sem,
            recv_sem=recv_sem,
            device_id=self.device(peer),
            device_id_type=pl.DeviceIdType.MESH,
        ).start()


def await_bytes(ref, sem):
    pltpu.make_async_copy(ref, ref, sem).wait()


def layer_kernel(
    shape, n_time, frame_group,
    vis_ref, tok_ref, attn_ref, in_hbm, out_hbm, virt_hbm, virtual_ref, dest_ref,
    time_ones, frame_ones, sort_ref, side_ref, home_ref, query_ref, in_ref, out_ref, virt_ref,
    slab, inbox, extra, x_ref, key_ref, value_ref, qb_ref, hub_ref, outbox,
    in_sem, out_sem, weight_sem, send1, recv1, local1, send_extra, recv_extra, local_extra,
    send_hub, recv_hub, send2, recv2, local2,
):
    step = pl.program_id(0)
    group, frames, feature = tok_ref.shape
    n_virtual = virtual_ref.shape[0]
    exchange = Exchange(shape)
    count, side = exchange.count, exchange.side
    local, here, there = exchange.local, exchange.here, exchange.there
    each = frames // count
    side_chunk = side * group
    own_tracks = n_time * group
    side_tracks = side * own_tracks
    lag = n_time - 3
    n_whole = n_time - DEFER
    short = each // 2
    pair = 2 * side_chunk

    @pl.when(step == 0)
    def _():
        pltpu.make_async_copy(in_hbm, in_ref, in_sem).start()
        pltpu.make_async_copy(out_hbm, out_ref, out_sem).start()
        exchange.greet()
        pltpu.make_async_copy(virt_hbm, virt_ref, weight_sem).start()
        fill_ones(time_ones, feature)

    def share(index, half):
        slot = index if half is None else half * n_time + index
        part = (slice(None),) if half is None else (half,)
        for j in range(side):
            peer = there + exchange.near(j)
            exchange.put(
                slab.at[(index, peer) + part], inbox.at[(index, side + local) + part], peer, send1, recv1.at[slot]
            )
        for j in exchange.offsets:
            peer = here + exchange.near(j)
            exchange.put(
                slab.at[(index, peer) + part], inbox.at[(index, local) + part], peer, send1, recv1.at[slot]
            )
        for j in exchange.offsets:
            near = exchange.near(j)
            exchange.put(
                slab.at[(index, there + near) + part], extra.at[(index, local) + part], here + near,
                send_extra, recv_extra.at[slot],
            )
        pltpu.make_async_copy(
            slab.at[(index, here + local) + part], inbox.at[(index, local) + part], local1.at[slot]
        ).start()
        pltpu.make_async_copy(
            slab.at[(index, there + local) + part], extra.at[(index, local) + part], local_extra.at[slot]
        ).start()

    def ready():
        @pl.when(step == 0)
        def _():
            pltpu.make_async_copy(in_hbm, in_ref, in_sem).wait()
            pltpu.make_async_copy(out_hbm, out_ref, out_sem).wait()

    @pl.when(step < n_time)
    def _():
        begin = [vis_ref[0, step * group + i] for i in range(group)]
        end = [vis_ref[1, step * group + i] for i in range(group)]
        after = time_step(tok_ref[...], begin, end, attn_ref, in_ref, out_ref, time_ones, ready)
        for half, block in enumerate(interleave(after[:frames], after[frames:], count)):
            slab[step, :, half] = block.astype(BF16)

        @pl.when(step == 0)
        def _():
            exchange.admit()

        @pl.when(step < n_whole)
        def _():
            share(step, None)

        if DEFER:
            @pl.when(step >= n_whole)
            def _():
                share(step, 0)

            @pl.when(step == n_time - 1)
            def _():
                for index in range(n_whole, n_time):
                    share(index, 1)

    @pl.when(step == lag)
    def _():
        pltpu.make_async_copy(virt_hbm, virt_ref, weight_sem).wait()
        query = project(layer_norm(virtual_ref[...]), virt_ref[0, 0]).astype(BF16)
        fill_ones(frame_ones, feature)
        for at, heads in enumerate(head_groups(feature)):
            query_ref[at] = spread_heads(query, head_masks(feature, BF16), heads)
        for ref, sides in ((sort_ref, 2), (side_ref, 1)):
            row = lax.broadcasted_iota(jnp.int32, ref.shape, 0)
            col = lax.broadcasted_iota(jnp.int32, ref.shape, 1)
            frame, track = row // (sides * pair), row % (sides * pair)
            far, track = track // pair, track % pair
            index, track = track // side_chunk, track % side_chunk
            sender = index * sides * side + far * side + track // group
            place = sender * each + track % group * short + frame
            ref[...] = jnp.where(col == place, 1.0, 0.0).astype(BF16)
        row = lax.broadcasted_iota(jnp.int32, home_ref.shape, 0)
        col = lax.broadcasted_iota(jnp.int32, home_ref.shape, 1)
        track = row % own_tracks
        place = track // group * side_chunk + row // own_tracks * group + track % group
        home_ref[...] = jnp.where(col == place, 1.0, 0.0).astype(BF16)

    def arrive(half, couple):
        whole, second = [], []
        for i in range(2):
            index = 2 * couple + i
            if index < n_whole:
                slot, part = index, ()
                if half:
                    continue
            else:
                slot, part = half * n_time + index, (half,)
            others = pl.ds(0, count - 1)
            near_others = pl.ds(0, side - 1)
            span = (slice(None),) if not part else part
            await_bytes(inbox.at[(index, others) + span], recv1.at[slot])
            await_bytes(inbox.at[(index, 0) + span], local1.at[slot])
            await_bytes(extra.at[(index, near_others) + span], recv_extra.at[slot])
            await_bytes(extra.at[(index, 0) + span], local_extra.at[slot])
        steps = slice(2 * couple, 2 * couple + 2)
        whole = project(sort_ref[...], inbox[steps, :, half].reshape(2 * count * each, feature)).astype(BF16)
        second = project(side_ref[...], extra[steps, :, half].reshape(2 * side * each, feature)).astype(BF16)
        normed = layer_norm(whole)
        second_normed = layer_norm(second).reshape(short, pair, feature)
        second = second.reshape(short, pair, feature)
        span = slice(half * short, (half + 1) * short)
        far_span = slice(each + half * short, each + (half + 1) * short)
        place = slice(2 * pair * couple, 2 * pair * (couple + 1))
        key_ref[span, place] = project(normed, virt_ref[0, 1]).astype(BF16).reshape(short, 2 * pair, feature)
        value_ref[span, place] = project(normed, virt_ref[0, 2]).astype(BF16).reshape(short, 2 * pair, feature)
        mine = whole.reshape(short, 2 * pair, feature)[:, :pair]
        mine_normed = normed.reshape(short, 2 * pair, feature)[:, :pair]
        both = jnp.concatenate([mine_normed, second_normed], axis=0).reshape(2 * short * pair, feature)
        query = project(both, virt_ref[2, 0]).astype(BF16).reshape(2 * short, pair, feature)
        place = slice(pair * couple, pair * (couple + 1))
        x_ref[span, place] = mine
        x_ref[far_span, place] = second
        qb_ref[span, place] = query[:short]
        qb_ref[far_span, place] = query[short:]

    def make_hub(part):
        span = pl.ds(part * frame_group, frame_group)
        hub_ref[0, part] = virtual_step(key_ref[span], value_ref[span], virt_ref, virtual_ref, query_ref)
        exchange.put(
            hub_ref.at[0, part], hub_ref.at[1, part], there + local, send_hub, recv_hub.at[part]
        )

    def give_back(which, part):
        first = which * each + part * frame_group
        span = pl.ds(first, frame_group)
        after = back_step(x_ref[span], qb_ref[span], hub_ref[which, part], virt_ref, frame_ones).astype(BF16)
        for f in range(frame_group):
            block = project(home_ref[...], after[f * side_tracks : (f + 1) * side_tracks]).astype(BF16)
            outbox[:, first + f] = block.reshape(side, own_tracks, feature)
        owner = (here if which == 0 else there) + local
        target = dest_ref.at[pl.ds(owner * each + part * frame_group, frame_group)]
        for j in exchange.offsets:
            near = exchange.near(j)
            exchange.put(outbox.at[near, span], target, here + near, send2, recv2)
        pltpu.make_async_copy(outbox.at[local, span], target, local2).start()

    for at, jobs in enumerate(make_plan(n_time)):
        @pl.when(step == at)
        def _(jobs=jobs):
            for kind, which, part in jobs:
                if kind == "arrive":
                    arrive(which, part)
                elif kind == "hub":
                    make_hub(part)
                else:
                    if which == 1:
                        await_bytes(hub_ref.at[1, part], recv_hub.at[part])
                    give_back(which, part)

    @pl.when(step == pl.num_programs(0) - 1)
    def _():
        await_bytes(slab.at[:, pl.ds(0, count - 1)], send1)
        await_bytes(slab.at[:, pl.ds(0, side - 1)], send_extra)
        await_bytes(hub_ref.at[0], send_hub)
        others = dest_ref.at[pl.ds(0, (side - 1) * 2 * each)]
        await_bytes(dest_ref.at[pl.ds(0, 2 * each)], local2)
        await_bytes(others, send2)
        await_bytes(others, recv2)


WHOLE = pl.BlockSpec(memory_space=pltpu.VMEM)
ANY = pl.BlockSpec(memory_space=pl.ANY)
DEFER = 1


def make_plan(n_time):
    couples = n_time // 2
    plan = [[] for _ in range(n_time - 1)]
    for couple in range(couples - 1):
        plan += [[("arrive", 0, couple)], [("arrive", 1, couple)]]
    plan += [[("arrive", 0, couples - 1)], [("hub", 0, 0)], [("back", 0, 0)]]
    plan += [[("arrive", 1, couples - 1)], [("hub", 0, 1)]]
    return plan + [[("back", 1, 0)], [("back", 0, 1)], [("back", 1, 1)]]


LIMIT = 60 * 1024 * 1024


def shards(shape, tokens, visible, time_attn, mlp_in, mlp_out, virt_attn, virtual):
    own_tracks, frames, feature = tokens.shape
    n_virtual = virtual.shape[0]
    count = shape["track"] * shape["sub"]
    side = count // 2
    each = frames // count
    group, frame_group = 2, each // 2
    n_time = own_tracks // group
    parts = each // frame_group
    dma = pltpu.SemaphoreType.DMA
    window = head_groups(feature)[0][1].stop
    result = pl.pallas_call(
        functools.partial(layer_kernel, shape, n_time, frame_group),
        grid=(len(make_plan(n_time)),),
        in_specs=[
            pl.BlockSpec(memory_space=pltpu.SMEM),
            pl.BlockSpec((group, frames, feature), lambda i: (jnp.minimum(i, n_time - 1), 0, 0)),
            WHOLE, ANY, ANY, ANY, WHOLE,
        ],
        out_specs=ANY,
        out_shape=jax.ShapeDtypeStruct((frames, own_tracks, feature), BF16),
        scratch_shapes=[
            pltpu.VMEM((2, HEADS // 2 * frames, window), BF16),
            pltpu.VMEM((2, HEADS // 2 * n_virtual, window), BF16),
            pltpu.VMEM((count * group * each, count * group * each), BF16),
            pltpu.VMEM((side * group * each, side * group * each), BF16),
            pltpu.VMEM((side * own_tracks, side * own_tracks), BF16),
            pltpu.VMEM((2, HEADS // 2 * n_virtual, window), BF16),
            pltpu.VMEM(mlp_in.shape, BF16),
            pltpu.VMEM(mlp_out.shape, BF16),
            pltpu.VMEM(virt_attn.shape, BF16),
            pltpu.VMEM((n_time, count, 2, each, feature), BF16),
            pltpu.VMEM((n_time, count, 2, each, feature), BF16),
            pltpu.VMEM((n_time, side, 2, each, feature), BF16),
            pltpu.VMEM((2 * each, side * own_tracks, feature), BF16),
            pltpu.VMEM((each, count * own_tracks, feature), BF16),
            pltpu.VMEM((each, count * own_tracks, feature), BF16),
            pltpu.VMEM((2 * each, side * own_tracks, feature), BF16),
            pltpu.VMEM((2, parts, frame_group * n_virtual, feature), BF16),
            pltpu.VMEM((side, 2 * each, own_tracks, feature), BF16),
            dma, dma, dma,
            dma, dma((2 * n_time,)), dma((2 * n_time,)),
            dma, dma((2 * n_time,)), dma((2 * n_time,)),
            dma, dma((parts,)),
            dma, dma, dma,
        ],
        compiler_params=pltpu.CompilerParams(vmem_limit_bytes=LIMIT, collective_id=0, has_side_effects=True),
    )(visible.T, tokens, time_attn, mlp_in, mlp_out, virt_attn, virtual)
    return jnp.swapaxes(result, 0, 1)


def solution(mesh):
    placed = (
        P(("groups", "track", "sub"), None, None),
        P(("groups", "track", "sub"), None),
        P(),
        P(),
        P(),
        P(),
        P(),
    )
    return jax.shard_map(
        functools.partial(shards, dict(mesh.shape)),
        mesh=mesh,
        in_specs=placed,
        out_specs=P(("groups", "track", "sub"), None, None),
        check_vma=False,
    )
```
